512 devices in a mesh: view: 8 (over y, x_lo), batch: 64 (over x_hi, z, core).
Axes of the slice: x: 4 (x_hi: 2, x_lo: 2; x = x_hi * 2 + x_lo), y: 4, z: 16, core: 2. Of those that a mesh axis runs over, the one named last changes fastest.
Arguments:
- embeddings: bfloat16 [8, 8192, 256], P('view', 'batch'), may hold values from -1.5 to 1.5
- positive: int32 [8, 8192], P(None, 'batch'), may hold values from 0 to 127, as said below
Outputs:
- gradients: float32 [8, 8192, 256], P('view', 'batch')
- totals: float32 [8, 8192], P('view', 'batch')
- row_loss: float32 [8, 8192], P('view', 'batch')
The draws below stay inside these ranges and needn't reach their ends.
Inputs may be any that keep to these rules, and one draw needn't show every extreme that they name: `positive`: for each view and each aligned block of 128 samples, the entries are a permutation of 0 to 127.
All inputs are finite; a program needn't handle non-finite values.
Results may differ from the reference program's by a relative error of at most 0.002.
Values may be sent and summed in bfloat16 or wider, within the bound.
No kernel may reach another device: no remote copies, remote signals or barrier semaphores. Data moves between devices by JAX's collectives and lax.ppermute only.
A program may use at most 64 MiB of HBM per device.

```python
import jax
import jax.numpy as jnp
from jax import lax

ROWS = 128
EMBED = 256
VIEWS = 8
BATCH = 8192


def draw_embeddings(key, part):
    normal_key = jax.random.fold_in(key, 0)
    values = jnp.clip(jax.random.normal(normal_key, (VIEWS, BATCH, EMBED), jnp.float32) * 0.11, -1.5, 1.5)
    return values.astype(jnp.bfloat16)


def draw_positive(key, part):
    shard_count = VIEWS * (BATCH // ROWS)
    key_list = jax.random.split(key, shard_count)
    orders = jax.vmap(lambda sub_key: jax.random.permutation(sub_key, ROWS))(key_list)
    return orders.reshape(VIEWS, BATCH).astype(jnp.int32)


def setup_inputs(seed: int = 0) -> dict:
    seeds = jax.random.split(jax.random.key(seed), 3)
    return {
        "embeddings": draw_embeddings(jax.random.fold_in(seeds[2], 71), 0),
        "positive": draw_positive(jax.random.fold_in(seeds[2], 71), 0),
    }


logit_scale = 10.0


def pair_terms(anchor_emb, key_emb):
    block_count = BATCH // ROWS
    block_ids = jnp.arange(block_count, dtype=jnp.int32)

    def block_scores(block_id):
        anchor_rows = lax.dynamic_slice_in_dim(anchor_emb, (block_id * ROWS).astype(jnp.int32), ROWS, 0)
        scores = jnp.dot(anchor_rows, key_emb.T, preferred_element_type=jnp.float32) * logit_scale
        return anchor_rows, scores

    def first_pass(running, block_id):
        column_max, column_sum = running
        anchor_rows, scores = block_scores(block_id)
        row_max = jnp.max(scores, axis=1, keepdims=True)
        row_total = row_max[:, 0] + jnp.log(jnp.sum(jnp.exp(scores - row_max), axis=1))
        new_max = jnp.maximum(column_max, jnp.max(scores, axis=0))
        column_sum = column_sum * jnp.exp(column_max - new_max) + jnp.sum(jnp.exp(scores - new_max[None, :]), axis=0)
        return (new_max, column_sum), row_total

    start_state = (jnp.full((BATCH,), -1e30, jnp.float32), jnp.zeros((BATCH,), jnp.float32))
    (column_max, column_sum), row_blocks = lax.scan(first_pass, start_state, block_ids)
    anchor_totals = row_blocks.reshape(BATCH)
    key_totals = column_max + jnp.log(column_sum)

    def second_pass(running, block_id):
        key_own, key_side = running
        anchor_rows, scores = block_scores(block_id)
        row_totals = lax.dynamic_slice_in_dim(anchor_totals, (block_id * ROWS).astype(jnp.int32), ROWS, 0)
        w_rows = jnp.exp(scores - row_totals[:, None]).astype(jnp.bfloat16)
        w_cols = jnp.exp(scores - key_totals[None, :]).astype(jnp.bfloat16)
        anchor_own = jnp.dot(w_rows, key_emb, preferred_element_type=jnp.float32)
        anchor_side = jnp.dot(w_cols, key_emb, preferred_element_type=jnp.float32)
        key_own = key_own + jnp.dot(w_cols.T, anchor_rows, preferred_element_type=jnp.float32)
        key_side = key_side + jnp.dot(w_rows.T, anchor_rows, preferred_element_type=jnp.float32)
        return (key_own, key_side), (anchor_own, anchor_side)

    zero_acc = jnp.zeros((BATCH, EMBED), jnp.float32)
    (key_own, key_side), (anchor_own, anchor_side) = lax.scan(second_pass, (zero_acc, zero_acc), block_ids)
    anchor_own = anchor_own.reshape(BATCH, EMBED)
    anchor_side = anchor_side.reshape(BATCH, EMBED)
    return anchor_totals, anchor_own, anchor_side, key_totals, key_own, key_side


def reference(embeddings, positive):
    half_views = VIEWS // 2
    totals_list = [None] * VIEWS
    own_list = [None] * VIEWS
    side_list = [None] * VIEWS
    for anchor_view in range(half_views):
        key_view = anchor_view + half_views
        results = pair_terms(embeddings[anchor_view], embeddings[key_view])
        totals_list[anchor_view], own_list[anchor_view], side_list[anchor_view] = results[0], results[1], results[2]
        totals_list[key_view], own_list[key_view], side_list[key_view] = results[3], results[4], results[5]
    block_base = (jnp.arange(BATCH, dtype=jnp.int32) // ROWS) * ROWS
    grad_list = []
    loss_list = []
    for view_id in range(VIEWS):
        paired = (view_id + half_views) % VIEWS
        match_own = block_base + positive[view_id].astype(jnp.int32)
        match_far = block_base + positive[paired].astype(jnp.int32)
        pos_rows = embeddings[paired][match_own].astype(jnp.float32)
        pos_score = jnp.sum(embeddings[view_id].astype(jnp.float32) * pos_rows, axis=1) * logit_scale
        loss_list.append(totals_list[view_id] - pos_score)
        matched = jnp.zeros((BATCH, EMBED), jnp.float32).at[match_far].add(embeddings[paired].astype(jnp.float32))
        grad_list.append(logit_scale * (own_list[view_id] - pos_rows + side_list[view_id] - matched))
    return jnp.stack(grad_list), jnp.stack(totals_list), jnp.stack(loss_list)
```

```python
import jax
import jax.numpy as jnp
from jax import lax
from jax.experimental import pallas as pl
from jax.experimental.pallas import tpu as pltpu
from jax.sharding import Mesh, PartitionSpec as P

logit_scale = 10.0

PAIR, REST = "pair", "rest"
XH, ZP, Z0, CORE = "xh", "zp", "z0", "core"
ROW_GROUP = (XH, Z0, CORE)
COL_GROUP = (ZP,)
VMEM = pl.BlockSpec(memory_space=pltpu.VMEM)


def score_block(rows, cols):
    return (
        lax.dot_general(rows, cols, (((1,), (1,)), ((), ())), preferred_element_type=jnp.float32)
        * logit_scale
    )


def combine(parts):
    top = jnp.max(parts, axis=0)
    return top + jnp.log(jnp.sum(jnp.exp(parts - top[None]), axis=0))


def lse_kernel(row_ref, col_ref, row_lse_ref, col_lse_ref, score_ref):
    step = 256
    for left, right, out in ((row_ref, col_ref, col_lse_ref), (col_ref, row_ref, row_lse_ref)):
        count, width = left.shape[0], right.shape[0]
        top = jnp.full((8, width), -1e30, jnp.float32)
        for start in range(0, count, step):
            block = score_block(left[start : start + step, :], right[...])
            score_ref[start : start + step, :] = block
            top = jnp.maximum(top, jnp.max(block.reshape(step // 8, 8, width), axis=0))
        top = jnp.max(top, axis=0, keepdims=True)
        total = jnp.zeros((8, width), jnp.float32)
        for start in range(0, count, step):
            block = jnp.exp(score_ref[start : start + step, :] - top)
            total = total + jnp.sum(block.reshape(step // 8, 8, width), axis=0)
        lse = top + jnp.log(jnp.sum(total, axis=0, keepdims=True))
        tile = jnp.concatenate([lse[:, i : i + 128] for i in range(0, width, 128)], axis=0)
        for peer in range(out.shape[0]):
            out[peer] = tile


def own_kernel(
    row_ref, col_ref, parts_ref, own_ref, partner_ref, positive_ref,
    grad_ref, totals_ref, loss_ref, base_ref, totals_scratch,
):
    totals = combine(parts_ref[...])
    totals_scratch[...] = totals
    block_rows = totals.shape[1]
    width = col_ref.shape[0]
    for i in range(totals.shape[0]):
        shift = jnp.broadcast_to(totals[i : i + 1, :], (128, block_rows)).T
        scores = score_block(row_ref[i * block_rows : (i + 1) * block_rows, :], col_ref[...])
        weights = jnp.exp(scores - jnp.concatenate([shift] * (width // 128), axis=1))
        grad_ref[i] = jnp.dot(
            weights.astype(jnp.bfloat16), col_ref[...], preferred_element_type=jnp.float32
        )
    rest_count = lax.axis_size(REST)
    pair = lax.axis_index(PAIR)
    view = pair * rest_count + lax.axis_index(REST)
    far = (1 - pair) * rest_count + lax.axis_index(REST)
    own_match = positive_ref[pl.ds(view, 1), :]
    far_match = positive_ref[pl.ds(far, 1), :]
    row_ids = lax.broadcasted_iota(jnp.int32, (block_rows, block_rows), 0)
    own_hot = (row_ids == own_match).astype(jnp.float32).astype(jnp.bfloat16)
    far_hot = (row_ids == far_match).astype(jnp.float32).astype(jnp.bfloat16)
    partner = partner_ref[...]
    pos_rows = lax.dot_general(
        own_hot, partner, (((0,), (0,)), ((), ())), preferred_element_type=jnp.float32
    )
    matched = jnp.dot(far_hot, partner, preferred_element_type=jnp.float32)
    base_ref[...] = (pos_rows + matched) * -logit_scale
    product = own_ref[...].astype(jnp.float32) * pos_rows
    pos_score = jnp.sum(product.T, axis=0, keepdims=True) * logit_scale
    place = (lax.axis_index(XH) * lax.axis_size(Z0) + lax.axis_index(Z0)) * lax.axis_size(CORE)
    place = place + lax.axis_index(CORE)
    own_totals = totals_scratch[pl.ds(place, 1), :]
    totals_ref[...] = own_totals
    loss_ref[...] = own_totals - pos_score


def side_kernel(row_ref, col_ref, parts_ref, own_grad_ref, grad_ref):
    totals = combine(parts_ref[...])
    shift = jnp.concatenate([totals[i : i + 1, :] for i in range(totals.shape[0])], axis=1)
    block_rows = grad_ref.shape[1]
    for i in range(grad_ref.shape[0]):
        scores = score_block(row_ref[i * block_rows : (i + 1) * block_rows, :], col_ref[...])
        weights = jnp.exp(scores - shift)
        grad_ref[i] = own_grad_ref[i] + jnp.dot(
            weights.astype(jnp.bfloat16), col_ref[...], preferred_element_type=jnp.float32
        )


def sum_kernel(parts_ref, base_ref, out_ref):
    total = parts_ref[0]
    for i in range(1, parts_ref.shape[0]):
        total = total + parts_ref[i]
    out_ref[...] = total * logit_scale + base_ref[...]


def call(kernel, outs, *args, flops=0, transcendentals=0, scratch=()):
    single = not isinstance(outs, tuple)
    out_list = (outs,) if single else outs
    moved = sum(a.size * a.dtype.itemsize for a in args)
    moved += sum(o.size * o.dtype.itemsize for o in out_list)
    return pl.pallas_call(
        kernel,
        out_shape=outs,
        in_specs=[VMEM] * len(args),
        out_specs=VMEM if single else tuple([VMEM] * len(out_list)),
        scratch_shapes=list(scratch),
        cost_estimate=pl.CostEstimate(
            flops=flops, bytes_accessed=moved, transcendentals=transcendentals
        ),
    )(*args)


def exchange(value, axes):
    return lax.all_to_all(value, axes, 0, 0, tiled=True)


def body(embeddings, positive):
    own = embeddings[0]
    row_count, width = own.shape
    rows_n = lax.axis_size(XH) * lax.axis_size(Z0) * lax.axis_size(CORE)
    cols_n = lax.axis_size(ZP)
    f32 = jnp.float32
    partner = lax.ppermute(own, PAIR, [(0, 1), (1, 0)])
    rows = exchange(jnp.broadcast_to(own[None], (rows_n, row_count, width)), ROW_GROUP)
    rows = rows.reshape(rows_n * row_count, width)
    cols = lax.all_gather(partner, COL_GROUP, axis=0, tiled=True)
    rows_total, cols_total = rows.shape[0], cols.shape[0]
    area = rows_total * cols_total
    row_parts, col_parts = call(
        lse_kernel,
        (
            jax.ShapeDtypeStruct((rows_n, rows_total // 128, 128), f32),
            jax.ShapeDtypeStruct((cols_n, cols_total // 128, 128), f32),
        ),
        rows, cols,
        flops=4 * area * width, transcendentals=2 * area,
        scratch=[pltpu.VMEM((max(rows_total, cols_total),) * 2, f32)],
    )
    row_parts = exchange(row_parts, ROW_GROUP)
    col_parts = exchange(col_parts, COL_GROUP)
    grads, totals, row_loss, base = call(
        own_kernel,
        (
            jax.ShapeDtypeStruct((rows_n, row_count, width), f32),
            jax.ShapeDtypeStruct((1, row_count), f32),
            jax.ShapeDtypeStruct((1, row_count), f32),
            jax.ShapeDtypeStruct((row_count, width), f32),
        ),
        rows, cols, row_parts, own, partner, positive,
        flops=4 * area * width, transcendentals=area,
        scratch=[pltpu.VMEM((rows_total // 128, 128), f32)],
    )
    grads = call(
        side_kernel,
        jax.ShapeDtypeStruct((rows_n, row_count, width), f32),
        rows, cols, col_parts, grads,
        flops=4 * area * width, transcendentals=area,
    )
    grads = exchange(grads, ROW_GROUP)
    gradients = call(sum_kernel, jax.ShapeDtypeStruct((row_count, width), f32), grads, base)
    return (gradients[None], totals, row_loss)


def solution(mesh):
    view, batch = mesh.shape["view"], mesh.shape["batch"]
    inner = Mesh(
        mesh.devices.reshape(2, view // 2, 2, batch // 8, 2, 2), (PAIR, REST, XH, ZP, Z0, CORE)
    )
    v, b = (PAIR, REST), (XH, ZP, Z0, CORE)
    return jax.shard_map(
        body,
        mesh=inner,
        in_specs=(P(v, b, None), P(None, b)),
        out_specs=(P(v, b, None), P(v, b), P(v, b)),
        check_vma=False,
    )
```

```python
import jax
import jax.numpy as jnp
from jax import lax
from jax.experimental import pallas as pl
from jax.experimental.pallas import tpu as pltpu
from jax.sharding import Mesh, PartitionSpec as P


logit_scale = 10.0

PAIR, REST = "pair", "rest"
XH, ZP, Z0, CORE = "xh", "zp", "z0", "core"
ROW_GROUP = (XH, Z0, CORE)
COL_GROUP = (ZP,)
VMEM = pl.BlockSpec(memory_space=pltpu.VMEM)


def score_block(rows, cols):
    return (
        lax.dot_general(rows, cols, (((1,), (1,)), ((), ())), preferred_element_type=jnp.float32)
        * logit_scale
    )


def combine(parts):
    top = jnp.max(parts, axis=0)
    return top + jnp.log(jnp.sum(jnp.exp(parts - top[None]), axis=0))


def lse_kernel(row_ref, col_ref, row_lse_ref, col_lse_ref, score_ref):
    step = 256
    for left, right, out in ((row_ref, col_ref, col_lse_ref), (col_ref, row_ref, row_lse_ref)):
        count, width = left.shape[0], right.shape[0]
        top = jnp.full((8, width), -1e30, jnp.float32)
        for start in range(0, count, step):
            block = score_block(left[start : start + step, :], right[...])
            score_ref[start : start + step, :] = block
            top = jnp.maximum(top, jnp.max(block.reshape(step // 8, 8, width), axis=0))
        top = jnp.max(top, axis=0, keepdims=True)
        total = jnp.zeros((8, width), jnp.float32)
        for start in range(0, count, step):
            block = jnp.exp(score_ref[start : start + step, :] - top)
            total = total + jnp.sum(block.reshape(step // 8, 8, width), axis=0)
        lse = top + jnp.log(jnp.sum(total, axis=0, keepdims=True))
        tile = jnp.concatenate([lse[:, i : i + 128] for i in range(0, width, 128)], axis=0)
        if len(out.shape) == 2:
            out[...] = tile
        else:
            for peer in range(out.shape[0]):
                out[peer] = tile


def own_kernel(
    row_ref, col_ref, parts_ref, own_ref, partner_ref, positive_ref,
    grad_ref, totals_ref, loss_ref, base_ref, totals_scratch,
):
    totals = combine(parts_ref[...])
    totals_scratch[...] = totals
    block_rows = totals.shape[1]
    width = col_ref.shape[0]
    for i in range(totals.shape[0]):
        shift = jnp.broadcast_to(totals[i : i + 1, :], (128, block_rows)).T
        scores = score_block(row_ref[i * block_rows : (i + 1) * block_rows, :], col_ref[...])
        weights = jnp.exp(scores - jnp.concatenate([shift] * (width // 128), axis=1))
        grad_ref[i] = jnp.dot(
            weights.astype(jnp.bfloat16), col_ref[...], preferred_element_type=jnp.float32
        )
    rest_count = lax.axis_size(REST)
    pair = lax.axis_index(PAIR)
    view = pair * rest_count + lax.axis_index(REST)
    far = (1 - pair) * rest_count + lax.axis_index(REST)
    own_match = positive_ref[pl.ds(view, 1), :]
    far_match = positive_ref[pl.ds(far, 1), :]
    row_ids = lax.broadcasted_iota(jnp.int32, (block_rows, block_rows), 0)
    own_hot = (row_ids == own_match).astype(jnp.float32).astype(jnp.bfloat16)
    far_hot = (row_ids == far_match).astype(jnp.float32).astype(jnp.bfloat16)
    partner = partner_ref[...]
    pos_rows = lax.dot_general(
        own_hot, partner, (((0,), (0,)), ((), ())), preferred_element_type=jnp.float32
    )
    matched = jnp.dot(far_hot, partner, preferred_element_type=jnp.float32)
    base_ref[...] = (pos_rows + matched) * -logit_scale
    product = own_ref[...].astype(jnp.float32) * pos_rows
    pos_score = jnp.sum(product.T, axis=0, keepdims=True) * logit_scale
    place = (lax.axis_index(XH) * lax.axis_size(Z0) + lax.axis_index(Z0)) * lax.axis_size(CORE)
    place = place + lax.axis_index(CORE)
    own_totals = totals_scratch[pl.ds(place, 1), :]
    totals_ref[...] = own_totals
    loss_ref[...] = own_totals - pos_score


def side_kernel(row_ref, col_ref, parts_ref, own_grad_ref, grad_ref):
    totals = combine(parts_ref[...])
    shift = jnp.concatenate([totals[i : i + 1, :] for i in range(totals.shape[0])], axis=1)
    block_rows = grad_ref.shape[1]
    for i in range(grad_ref.shape[0]):
        scores = score_block(row_ref[i * block_rows : (i + 1) * block_rows, :], col_ref[...])
        weights = jnp.exp(scores - shift)
        grad_ref[i] = own_grad_ref[i] + jnp.dot(
            weights.astype(jnp.bfloat16), col_ref[...], preferred_element_type=jnp.float32
        )


def sum_kernel(parts_ref, base_ref, out_ref):
    total = parts_ref[0]
    for i in range(1, parts_ref.shape[0]):
        total = total + parts_ref[i]
    out_ref[...] = total * logit_scale + base_ref[...]


def call(kernel, outs, *args, flops=0, transcendentals=0, scratch=()):
    single = not isinstance(outs, tuple)
    out_list = (outs,) if single else outs
    moved = sum(a.size * a.dtype.itemsize for a in args)
    moved += sum(o.size * o.dtype.itemsize for o in out_list)
    return pl.pallas_call(
        kernel,
        out_shape=outs,
        in_specs=[VMEM] * len(args),
        out_specs=VMEM if single else tuple([VMEM] * len(out_list)),
        scratch_shapes=list(scratch),
        compiler_params=pltpu.CompilerParams(vmem_limit_bytes=16 << 20),
        cost_estimate=pl.CostEstimate(
            flops=flops, bytes_accessed=moved, transcendentals=transcendentals
        ),
    )(*args)


def exchange(value, axes):
    return lax.all_to_all(value, axes, 0, 0, tiled=True)


def step(embeddings, positive):
    own = embeddings[0]
    row_count, width = own.shape
    rows_n = lax.axis_size(XH) * lax.axis_size(Z0) * lax.axis_size(CORE)
    cols_n = lax.axis_size(ZP)
    f32 = jnp.float32
    partner = lax.ppermute(own, PAIR, [(0, 1), (1, 0)])
    rows = exchange(jnp.broadcast_to(own[None], (rows_n, row_count, width)), ROW_GROUP)
    rows = rows.reshape(rows_n * row_count, width)
    cols = lax.all_gather(partner, COL_GROUP, axis=0, tiled=True)
    rows_total, cols_total = rows.shape[0], cols.shape[0]
    area = rows_total * cols_total
    row_parts, col_parts = call(
        lse_kernel,
        (
            jax.ShapeDtypeStruct((rows_total // 128, 128), f32),
            jax.ShapeDtypeStruct((cols_n, cols_total // 128, 128), f32),
        ),
        rows, cols,
        flops=4 * area * width, transcendentals=2 * area,
        scratch=[pltpu.VMEM((max(rows_total, cols_total),) * 2, f32)],
    )
    row_parts = lax.all_gather(row_parts, ROW_GROUP, axis=0, tiled=False)
    col_parts = exchange(col_parts, COL_GROUP)
    grads, totals, row_loss, base = call(
        own_kernel,
        (
            jax.ShapeDtypeStruct((rows_n, row_count, width), f32),
            jax.ShapeDtypeStruct((1, row_count), f32),
            jax.ShapeDtypeStruct((1, row_count), f32),
            jax.ShapeDtypeStruct((row_count, width), f32),
        ),
        rows, cols, row_parts, own, partner, positive,
        flops=4 * area * width, transcendentals=area,
        scratch=[pltpu.VMEM((rows_total // 128, 128), f32)],
    )
    grads = call(
        side_kernel,
        jax.ShapeDtypeStruct((rows_n, row_count, width), f32),
        rows, cols, col_parts, grads,
        flops=4 * area * width, transcendentals=area,
    )
    grads = exchange(grads, ROW_GROUP)
    gradients = call(sum_kernel, jax.ShapeDtypeStruct((row_count, width), f32), grads, base)
    return (gradients[None], totals, row_loss)


def solution(mesh):
    view, batch = mesh.shape["view"], mesh.shape["batch"]
    inner = Mesh(
        mesh.devices.reshape(2, view // 2, 2, batch // 8, 2, 2), (PAIR, REST, XH, ZP, Z0, CORE)
    )
    v, b = (PAIR, REST), (XH, ZP, Z0, CORE)
    return jax.shard_map(
        step,
        mesh=inner,
        in_specs=(P(v, b, None), P(None, b)),
        out_specs=(P(v, b, None), P(v, b), P(v, b)),
        check_vma=False,
    )
```

```python
import functools

import jax
import jax.numpy as jnp
from jax import lax
from jax.experimental import pallas as pl
from jax.experimental.pallas import tpu as pltpu
from jax.sharding import Mesh, PartitionSpec as P


logit_scale = 10.0

PAIR, REST = "pair", "rest"
XH, ZP, Z0, CORE = "xh", "zp", "z0", "core"
ROW_GROUP = (XH, Z0, CORE)
COL_GROUP = (ZP,)
VMEM = pl.BlockSpec(memory_space=pltpu.VMEM)


def score_block(rows, cols):
    return (
        lax.dot_general(rows, cols, (((1,), (1,)), ((), ())), preferred_element_type=jnp.float32)
        * logit_scale
    )


def combine(parts):
    top = jnp.max(parts, axis=0)
    return top + jnp.log(jnp.sum(jnp.exp(parts - top[None]), axis=0))


def lse_kernel(row_ref, col_ref, row_lse_ref, col_lse_ref, score_ref):
    step = 256
    for left, right, out in ((row_ref, col_ref, col_lse_ref), (col_ref, row_ref, row_lse_ref)):
        count, width = left.shape[0], right.shape[0]
        top = jnp.full((8, width), -1e30, jnp.float32)
        for start in range(0, count, step):
            block = score_block(left[start : start + step, :], right[...])
            score_ref[start : start + step, :] = block
            top = jnp.maximum(top, jnp.max(block.reshape(step // 8, 8, width), axis=0))
        top = jnp.max(top, axis=0, keepdims=True)
        total = jnp.zeros((8, width), jnp.float32)
        for start in range(0, count, step):
            block = jnp.exp(score_ref[start : start + step, :] - top)
            total = total + jnp.sum(block.reshape(step // 8, 8, width), axis=0)
        lse = top + jnp.log(jnp.sum(total, axis=0, keepdims=True))
        tile = jnp.concatenate([lse[:, i : i + 128] for i in range(0, width, 128)], axis=0)
        if len(out.shape) == 2:
            out[...] = tile
        else:
            for peer in range(out.shape[0]):
                out[peer] = tile


def own_kernel(
    row_ref, col_ref, parts_ref, own_ref, partner_ref, positive_ref,
    grad_ref, totals_ref, loss_ref, base_ref, totals_scratch,
):
    groups, halves, tile_rows, lanes = parts_ref.shape
    totals = combine(parts_ref[...].reshape(groups * halves, tile_rows, lanes))
    totals_scratch[...] = totals
    block_rows = totals.shape[1]
    width = col_ref.shape[0]
    for i in range(totals.shape[0]):
        shift = jnp.broadcast_to(totals[i : i + 1, :], (128, block_rows)).T
        scores = score_block(row_ref[i * block_rows : (i + 1) * block_rows, :], col_ref[...])
        weights = jnp.exp(scores - jnp.concatenate([shift] * (width // 128), axis=1))
        grad_ref[i] = jnp.dot(
            weights.astype(jnp.bfloat16), col_ref[...], preferred_element_type=jnp.float32
        )
    rest_count = lax.axis_size(REST)
    pair = lax.axis_index(PAIR)
    view = pair * rest_count + lax.axis_index(REST)
    far = (1 - pair) * rest_count + lax.axis_index(REST)
    own_match = positive_ref[pl.ds(view, 1), :]
    far_match = positive_ref[pl.ds(far, 1), :]
    row_ids = lax.broadcasted_iota(jnp.int32, (block_rows, block_rows), 0)
    own_hot = (row_ids == own_match).astype(jnp.float32).astype(jnp.bfloat16)
    far_hot = (row_ids == far_match).astype(jnp.float32).astype(jnp.bfloat16)
    partner = partner_ref[...]
    pos_rows = lax.dot_general(
        own_hot, partner, (((0,), (0,)), ((), ())), preferred_element_type=jnp.float32
    )
    matched = jnp.dot(far_hot, partner, preferred_element_type=jnp.float32)
    base_ref[...] = (pos_rows + matched) * -logit_scale
    product = own_ref[...].astype(jnp.float32) * pos_rows
    pos_score = jnp.sum(product.T, axis=0, keepdims=True) * logit_scale
    place = (lax.axis_index(XH) * lax.axis_size(Z0) + lax.axis_index(Z0)) * lax.axis_size(CORE)
    place = place + lax.axis_index(CORE)
    own_totals = totals_scratch[pl.ds(place, 1), :]
    totals_ref[...] = own_totals
    loss_ref[...] = own_totals - pos_score


def side_kernel(flip, row_ref, col_ref, parts_ref, own_grad_ref, grad_ref):
    totals = combine(parts_ref[...])
    shift = jnp.concatenate([totals[i : i + 1, :] for i in range(totals.shape[0])], axis=1)
    block_rows = grad_ref.shape[1]
    cores = lax.axis_size(CORE)
    core = lax.rem(lax.axis_index(CORE) + flip, cores)
    for i in range(grad_ref.shape[0]):
        block = i * cores + core
        start = pl.multiple_of(block * block_rows, block_rows)
        scores = score_block(row_ref[pl.ds(start, block_rows), :], col_ref[...])
        weights = jnp.exp(scores - shift)
        grad_ref[i] = own_grad_ref[block] + jnp.dot(
            weights.astype(jnp.bfloat16), col_ref[...], preferred_element_type=jnp.float32
        )


def sum_kernel(parts_ref, base_ref, out_ref):
    total = parts_ref[0]
    for i in range(1, parts_ref.shape[0]):
        total = total + parts_ref[i]
    out_ref[...] = total * logit_scale + base_ref[...]


def call(kernel, outs, *args, flops=0, transcendentals=0, scratch=()):
    single = not isinstance(outs, tuple)
    out_list = (outs,) if single else outs
    moved = sum(a.size * a.dtype.itemsize for a in args)
    moved += sum(o.size * o.dtype.itemsize for o in out_list)
    return pl.pallas_call(
        kernel,
        out_shape=outs,
        in_specs=[VMEM] * len(args),
        out_specs=VMEM if single else tuple([VMEM] * len(out_list)),
        scratch_shapes=list(scratch),
        compiler_params=pltpu.CompilerParams(vmem_limit_bytes=16 << 20),
        cost_estimate=pl.CostEstimate(
            flops=flops, bytes_accessed=moved, transcendentals=transcendentals
        ),
    )(*args)


def exchange(value, axes):
    return lax.all_to_all(value, axes, 0, 0, tiled=True)


def step(embeddings, positive):
    own = embeddings[0]
    row_count, width = own.shape
    rows_n = lax.axis_size(XH) * lax.axis_size(Z0) * lax.axis_size(CORE)
    cols_n = lax.axis_size(ZP)
    f32 = jnp.float32
    partner = lax.ppermute(own, PAIR, [(0, 1), (1, 0)])
    rows = exchange(jnp.broadcast_to(own[None], (rows_n, row_count, width)), ROW_GROUP)
    rows = rows.reshape(rows_n * row_count, width)
    cols = lax.all_gather(partner, COL_GROUP, axis=0, tiled=True)
    rows_total, cols_total = rows.shape[0], cols.shape[0]
    area = rows_total * cols_total
    row_parts, col_parts = call(
        lse_kernel,
        (
            jax.ShapeDtypeStruct((rows_total // 128, 128), f32),
            jax.ShapeDtypeStruct((cols_n, cols_total // 128, 128), f32),
        ),
        rows, cols,
        flops=4 * area * width, transcendentals=2 * area,
        scratch=[pltpu.VMEM((max(rows_total, cols_total),) * 2, f32)],
    )
    far_parts = lax.ppermute(row_parts, Z0, [(0, 1), (1, 0)])
    row_parts = lax.all_gather(jnp.stack([row_parts, far_parts]), (XH, CORE), axis=0, tiled=False)
    col_parts = exchange(col_parts, COL_GROUP)
    grads, totals, row_loss, base = call(
        own_kernel,
        (
            jax.ShapeDtypeStruct((rows_n, row_count, width), f32),
            jax.ShapeDtypeStruct((1, row_count), f32),
            jax.ShapeDtypeStruct((1, row_count), f32),
            jax.ShapeDtypeStruct((row_count, width), f32),
        ),
        rows, cols, row_parts, own, partner, positive,
        flops=4 * area * width, transcendentals=area,
        scratch=[pltpu.VMEM((rows_total // 128, 128), f32)],
    )
    halves = [
        call(
            functools.partial(side_kernel, flip),
            jax.ShapeDtypeStruct((rows_n // 2, row_count, width), f32),
            rows, cols, col_parts, grads,
            flops=2 * area * width, transcendentals=area // 2,
        )
        for flip in (1, 0)
    ]
    received = lax.ppermute(halves[0], CORE, [(0, 1), (1, 0)])
    grads = exchange(halves[1] + received, (XH, Z0))
    gradients = call(sum_kernel, jax.ShapeDtypeStruct((row_count, width), f32), grads, base)
    return (gradients[None], totals, row_loss)


def solution(mesh):
    view, batch = mesh.shape["view"], mesh.shape["batch"]
    inner = Mesh(
        mesh.devices.reshape(2, view // 2, 2, batch // 8, 2, 2), (PAIR, REST, XH, ZP, Z0, CORE)
    )
    v, b = (PAIR, REST), (XH, ZP, Z0, CORE)
    return jax.shard_map(
        step,
        mesh=inner,
        in_specs=(P(v, b, None), P(None, b)),
        out_specs=(P(v, b, None), P(v, b), P(v, b)),
        check_vma=False,
    )
```

```python
import functools

import jax
import jax.numpy as jnp
from jax import lax
from jax.experimental import pallas as pl
from jax.experimental.pallas import tpu as pltpu
from jax.sharding import Mesh, PartitionSpec as P


logit_scale = 10.0
log2_e = 1.4426950408889634
ln_2 = 0.6931471805599453

PAIR, REST = "pair", "rest"
XH, ZP, Z0, CORE = "xh", "zp", "z0", "core"
ROW_GROUP = (XH, Z0, CORE)
COL_GROUP = (ZP, CORE)
VMEM = pl.BlockSpec(memory_space=pltpu.VMEM)


def score_block(rows, cols):
    return lax.dot_general(
        rows, cols, (((1,), (1,)), ((), ())), preferred_element_type=jnp.float32
    ) * (logit_scale * log2_e)


def combine(parts):
    top = jnp.max(parts, axis=0)
    return top + jnp.log(jnp.sum(jnp.exp2(parts - top[None]), axis=0)) * log2_e


def lse_kernel(row_ref, col_ref, row_lse_ref, col_lse_ref, score_ref):
    step = 256
    for left, right, out in ((row_ref, col_ref, col_lse_ref), (col_ref, row_ref, row_lse_ref)):
        count, width = left.shape[0], right.shape[0]
        top = jnp.full((8, width), -1e30, jnp.float32)
        for start in range(0, count, step):
            block = score_block(left[start : start + step, :], right[...])
            score_ref[start : start + step, :] = block
            top = jnp.maximum(top, jnp.max(block.reshape(step // 8, 8, width), axis=0))
        top = jnp.max(top, axis=0, keepdims=True)
        total = jnp.zeros((8, width), jnp.float32)
        for start in range(0, count, step):
            block = jnp.exp2(score_ref[start : start + step, :] - top)
            total = total + jnp.sum(block.reshape(step // 8, 8, width), axis=0)
        lse = top + jnp.log(jnp.sum(total, axis=0, keepdims=True)) * log2_e
        tile = jnp.concatenate([lse[:, i : i + 128] for i in range(0, width, 128)], axis=0)
        if len(out.shape) == 2:
            out[...] = tile
        else:
            for peer in range(out.shape[0]):
                out[peer] = tile


def own_kernel(
    row_ref, col_ref, parts_ref, own_ref, partner_ref, positive_ref,
    grad_ref, totals_ref, loss_ref, base_ref, totals_scratch,
):
    groups, halves, tile_rows, lanes = parts_ref.shape
    totals = combine(parts_ref[...].reshape(groups * halves, tile_rows, lanes))
    totals_scratch[...] = totals
    block_rows = totals.shape[1]
    width = col_ref.shape[0]
    for i in range(totals.shape[0]):
        shift = jnp.broadcast_to(totals[i : i + 1, :], (128, block_rows)).T
        scores = score_block(row_ref[i * block_rows : (i + 1) * block_rows, :], col_ref[...])
        weights = jnp.exp2(scores - jnp.concatenate([shift] * (width // 128), axis=1))
        grad_ref[i] = jnp.dot(
            weights.astype(jnp.bfloat16), col_ref[...], preferred_element_type=jnp.float32
        )
    rest_count = lax.axis_size(REST)
    pair = lax.axis_index(PAIR)
    view = pair * rest_count + lax.axis_index(REST)
    far = (1 - pair) * rest_count + lax.axis_index(REST)
    own_match = positive_ref[pl.ds(view, 1), :]
    far_match = positive_ref[pl.ds(far, 1), :]
    row_ids = lax.broadcasted_iota(jnp.int32, (block_rows, block_rows), 0)
    own_hot = (row_ids == own_match).astype(jnp.float32).astype(jnp.bfloat16)
    far_hot = (row_ids == far_match).astype(jnp.float32).astype(jnp.bfloat16)
    partner = partner_ref[...]
    pos_rows = lax.dot_general(
        own_hot, partner, (((0,), (0,)), ((), ())), preferred_element_type=jnp.float32
    )
    matched = jnp.dot(far_hot, partner, preferred_element_type=jnp.float32)
    base_ref[...] = (pos_rows + matched) * -logit_scale
    product = own_ref[...].astype(jnp.float32) * pos_rows
    pos_score = jnp.sum(product.T, axis=0, keepdims=True) * logit_scale
    place = (lax.axis_index(XH) * lax.axis_size(Z0) + lax.axis_index(Z0)) * lax.axis_size(CORE)
    place = place + lax.axis_index(CORE)
    own_totals = totals_scratch[pl.ds(place, 1), :] * ln_2
    totals_ref[...] = own_totals
    loss_ref[...] = own_totals - pos_score


def side_kernel(flip, row_ref, col_ref, parts_ref, own_grad_ref, grad_ref):
    totals = combine(parts_ref[...])
    shift = jnp.concatenate([totals[i : i + 1, :] for i in range(totals.shape[0])], axis=1)
    block_rows = grad_ref.shape[1]
    cores = lax.axis_size(CORE)
    core = lax.rem(lax.axis_index(CORE) + flip, cores)
    for i in range(grad_ref.shape[0]):
        block = i * cores + core
        start = pl.multiple_of(block * block_rows, block_rows)
        scores = score_block(row_ref[pl.ds(start, block_rows), :], col_ref[...])
        weights = jnp.exp2(scores - shift)
        grad_ref[i] = own_grad_ref[block] + jnp.dot(
            weights.astype(jnp.bfloat16), col_ref[...], preferred_element_type=jnp.float32
        )


def sum_kernel(parts_ref, base_ref, out_ref):
    total = parts_ref[0]
    for i in range(1, parts_ref.shape[0]):
        total = total + parts_ref[i]
    out_ref[...] = total * logit_scale + base_ref[...]


def call(kernel, outs, *args, flops=0, transcendentals=0, scratch=()):
    single = not isinstance(outs, tuple)
    out_list = (outs,) if single else outs
    moved = sum(a.size * a.dtype.itemsize for a in args)
    moved += sum(o.size * o.dtype.itemsize for o in out_list)
    return pl.pallas_call(
        kernel,
        out_shape=outs,
        in_specs=[VMEM] * len(args),
        out_specs=VMEM if single else tuple([VMEM] * len(out_list)),
        scratch_shapes=list(scratch),
        compiler_params=pltpu.CompilerParams(vmem_limit_bytes=16 << 20),
        cost_estimate=pl.CostEstimate(
            flops=flops, bytes_accessed=moved, transcendentals=transcendentals
        ),
    )(*args)


def col_groups():
    planes, cores = lax.axis_size(ZP), lax.axis_size(CORE)
    return [[p * cores + (p + g) % cores for p in range(planes)] for g in range(cores)]


def exchange(value, axes, groups=None):
    return lax.all_to_all(value, axes, 0, 0, tiled=True, axis_index_groups=groups)


def step(embeddings, positive):
    own = embeddings[0]
    row_count, width = own.shape
    rows_n = lax.axis_size(XH) * lax.axis_size(Z0) * lax.axis_size(CORE)
    cols_n = lax.axis_size(ZP)
    f32 = jnp.float32
    partner = lax.ppermute(own, PAIR, [(0, 1), (1, 0)])
    rows = exchange(jnp.broadcast_to(own[None], (rows_n, row_count, width)), ROW_GROUP)
    rows = rows.reshape(rows_n * row_count, width)
    cols = lax.all_gather(partner, COL_GROUP, axis=0, tiled=True, axis_index_groups=col_groups())
    rows_total, cols_total = rows.shape[0], cols.shape[0]
    area = rows_total * cols_total
    row_parts, col_parts = call(
        lse_kernel,
        (
            jax.ShapeDtypeStruct((rows_total // 128, 128), f32),
            jax.ShapeDtypeStruct((cols_n, cols_total // 128, 128), f32),
        ),
        rows, cols,
        flops=4 * area * width, transcendentals=2 * area,
        scratch=[pltpu.VMEM((max(rows_total, cols_total),) * 2, f32)],
    )
    far_parts = lax.ppermute(row_parts, Z0, [(0, 1), (1, 0)])
    row_parts = lax.all_gather(jnp.stack([row_parts, far_parts]), (XH, CORE), axis=0, tiled=False)
    col_parts = exchange(col_parts, COL_GROUP, col_groups())
    grads, totals, row_loss, base = call(
        own_kernel,
        (
            jax.ShapeDtypeStruct((rows_n, row_count, width), f32),
            jax.ShapeDtypeStruct((1, row_count), f32),
            jax.ShapeDtypeStruct((1, row_count), f32),
            jax.ShapeDtypeStruct((row_count, width), f32),
        ),
        rows, cols, row_parts, own, partner, positive,
        flops=4 * area * width, transcendentals=area,
        scratch=[pltpu.VMEM((rows_total // 128, 128), f32)],
    )
    halves = [
        call(
            functools.partial(side_kernel, flip),
            jax.ShapeDtypeStruct((rows_n // 2, row_count, width), f32),
            rows, cols, col_parts, grads,
            flops=2 * area * width, transcendentals=area // 2,
        )
        for flip in (1, 0)
    ]
    received = lax.ppermute(halves[0], CORE, [(0, 1), (1, 0)])
    grads = exchange(halves[1] + received, (XH, Z0))
    gradients = call(sum_kernel, jax.ShapeDtypeStruct((row_count, width), f32), grads, base)
    return (gradients[None], totals, row_loss)


def solution(mesh):
    view, batch = mesh.shape["view"], mesh.shape["batch"]
    inner = Mesh(
        mesh.devices.reshape(2, view // 2, 2, batch // 8, 2, 2), (PAIR, REST, XH, ZP, Z0, CORE)
    )
    v, b = (PAIR, REST), (XH, ZP, Z0, CORE)
    return jax.shard_map(
        step,
        mesh=inner,
        in_specs=(P(v, b, None), P(None, b)),
        out_specs=(P(v, b, None), P(v, b), P(v, b)),
        check_vma=False,
    )
```

```python
import functools

import jax
import jax.numpy as jnp
from jax import lax
from jax.experimental import pallas as pl
from jax.experimental.pallas import tpu as pltpu
from jax.sharding import Mesh, PartitionSpec as P


logit_scale = 10.0
log2_e = 1.4426950408889634
ln_2 = 0.6931471805599453

PAIR, REST = "pair", "rest"
XH, ZP, Z0, CORE = "xh", "zp", "z0", "core"
ROW_GROUP = (XH, Z0, CORE)
COL_GROUP = (ZP, CORE)
BATCHED = 4
VMEM = pl.BlockSpec(memory_space=pltpu.VMEM)


def score_block(rows, cols):
    return lax.dot_general(
        rows, cols, (((1,), (1,)), ((), ())), preferred_element_type=jnp.float32
    ) * (logit_scale * log2_e)


def combine(parts):
    top = jnp.max(parts, axis=0)
    return top + jnp.log(jnp.sum(jnp.exp2(parts - top[None]), axis=0)) * log2_e


def lse_kernel(row_ref, col_ref, row_lse_ref, col_lse_ref, score_ref):
    step = 512
    for left, right, out in ((row_ref, col_ref, col_lse_ref), (col_ref, row_ref, row_lse_ref)):
        count, width = left.shape[0], right.shape[0]
        top = jnp.full((8, width), -1e30, jnp.float32)
        for start in range(0, count, step):
            block = score_block(left[start : start + step, :], right[...])
            score_ref[start : start + step, :] = block
            top = jnp.maximum(top, jnp.max(block.reshape(step // 8, 8, width), axis=0))
        top = jnp.max(top, axis=0, keepdims=True)
        total = jnp.zeros((8, width), jnp.float32)
        for start in range(0, count, step):
            block = jnp.exp2(score_ref[start : start + step, :] - top)
            total = total + jnp.sum(block.reshape(step // 8, 8, width), axis=0)
        lse = top + jnp.log(jnp.sum(total, axis=0, keepdims=True)) * log2_e
        tile = jnp.concatenate([lse[:, i : i + 128] for i in range(0, width, 128)], axis=0)
        if len(out.shape) == 2:
            out[...] = tile
        else:
            for peer in range(out.shape[0]):
                out[peer] = tile


def own_kernel(
    row_ref, col_ref, parts_ref, own_ref, partner_ref, positive_ref,
    grad_ref, totals_ref, loss_ref, base_ref, totals_scratch,
):
    groups, halves, tile_rows, lanes = parts_ref.shape
    totals = combine(parts_ref[...].reshape(groups * halves, tile_rows, lanes))
    totals_scratch[...] = totals
    block_rows = totals.shape[1]
    tiles = col_ref.shape[0] // 128
    for first in range(0, totals.shape[0], BATCHED):
        shift = jnp.concatenate(
            [
                jnp.broadcast_to(totals[i : i + 1, :], (128, block_rows)).T
                for i in range(first, first + BATCHED)
            ],
            axis=0,
        )
        rows = row_ref[first * block_rows : (first + BATCHED) * block_rows, :]
        scores = score_block(rows, col_ref[...])
        weights = jnp.exp2(scores - jnp.concatenate([shift] * tiles, axis=1))
        part = jnp.dot(
            weights.astype(jnp.bfloat16), col_ref[...], preferred_element_type=jnp.float32
        )
        grad_ref[first : first + BATCHED] = part.reshape(BATCHED, block_rows, part.shape[1])
    rest_count = lax.axis_size(REST)
    pair = lax.axis_index(PAIR)
    view = pair * rest_count + lax.axis_index(REST)
    far = (1 - pair) * rest_count + lax.axis_index(REST)
    own_match = positive_ref[pl.ds(view, 1), :]
    far_match = positive_ref[pl.ds(far, 1), :]
    row_ids = lax.broadcasted_iota(jnp.int32, (block_rows, block_rows), 0)
    own_hot = (row_ids == own_match).astype(jnp.float32).astype(jnp.bfloat16)
    far_hot = (row_ids == far_match).astype(jnp.float32).astype(jnp.bfloat16)
    partner = partner_ref[...]
    pos_rows = lax.dot_general(
        own_hot, partner, (((0,), (0,)), ((), ())), preferred_element_type=jnp.float32
    )
    matched = jnp.dot(far_hot, partner, preferred_element_type=jnp.float32)
    base_ref[...] = (pos_rows + matched) * -logit_scale
    product = own_ref[...].astype(jnp.float32) * pos_rows
    pos_score = jnp.sum(product.T, axis=0, keepdims=True) * logit_scale
    place = (lax.axis_index(XH) * lax.axis_size(Z0) + lax.axis_index(Z0)) * lax.axis_size(CORE)
    place = place + lax.axis_index(CORE)
    own_totals = totals_scratch[pl.ds(place, 1), :] * ln_2
    totals_ref[...] = own_totals
    loss_ref[...] = own_totals - pos_score


def side_kernel(flip, row_ref, col_ref, parts_ref, own_grad_ref, grad_ref):
    totals = combine(parts_ref[...])
    shift = jnp.concatenate([totals[i : i + 1, :] for i in range(totals.shape[0])], axis=1)
    block_rows = grad_ref.shape[1]
    cores = lax.axis_size(CORE)
    core = lax.rem(lax.axis_index(CORE) + flip, cores)
    blocks = [i * cores + core for i in range(grad_ref.shape[0])]
    rows = jnp.concatenate(
        [row_ref[pl.ds(pl.multiple_of(k * block_rows, block_rows), block_rows), :] for k in blocks],
        axis=0,
    )
    weights = jnp.exp2(score_block(rows, col_ref[...]) - shift)
    part = jnp.dot(weights.astype(jnp.bfloat16), col_ref[...], preferred_element_type=jnp.float32)
    for i, k in enumerate(blocks):
        grad_ref[i] = own_grad_ref[k] + part[i * block_rows : (i + 1) * block_rows, :]


def sum_kernel(parts_ref, base_ref, out_ref):
    total = parts_ref[0]
    for i in range(1, parts_ref.shape[0]):
        total = total + parts_ref[i]
    out_ref[...] = total * logit_scale + base_ref[...]


def call(kernel, outs, *args, flops=0, transcendentals=0, scratch=()):
    single = not isinstance(outs, tuple)
    out_list = (outs,) if single else outs
    moved = sum(a.size * a.dtype.itemsize for a in args)
    moved += sum(o.size * o.dtype.itemsize for o in out_list)
    return pl.pallas_call(
        kernel,
        out_shape=outs,
        in_specs=[VMEM] * len(args),
        out_specs=VMEM if single else tuple([VMEM] * len(out_list)),
        scratch_shapes=list(scratch),
        compiler_params=pltpu.CompilerParams(vmem_limit_bytes=16 << 20),
        cost_estimate=pl.CostEstimate(
            flops=flops, bytes_accessed=moved, transcendentals=transcendentals
        ),
    )(*args)


def col_groups():
    planes, cores = lax.axis_size(ZP), lax.axis_size(CORE)
    return [[p * cores + (p + g) % cores for p in range(planes)] for g in range(cores)]


def exchange(value, axes, groups=None):
    return lax.all_to_all(value, axes, 0, 0, tiled=True, axis_index_groups=groups)


def step(embeddings, positive):
    own = embeddings[0]
    row_count, width = own.shape
    rows_n = lax.axis_size(XH) * lax.axis_size(Z0) * lax.axis_size(CORE)
    cols_n = lax.axis_size(ZP)
    f32 = jnp.float32
    partner = lax.ppermute(own, PAIR, [(0, 1), (1, 0)])
    rows = exchange(jnp.broadcast_to(own[None], (rows_n, row_count, width)), ROW_GROUP)
    rows = rows.reshape(rows_n * row_count, width)
    cols = lax.all_gather(partner, COL_GROUP, axis=0, tiled=True, axis_index_groups=col_groups())
    rows_total, cols_total = rows.shape[0], cols.shape[0]
    area = rows_total * cols_total
    row_parts, col_parts = call(
        lse_kernel,
        (
            jax.ShapeDtypeStruct((rows_total // 128, 128), f32),
            jax.ShapeDtypeStruct((cols_n, cols_total // 128, 128), f32),
        ),
        rows, cols,
        flops=4 * area * width, transcendentals=2 * area,
        scratch=[pltpu.VMEM((max(rows_total, cols_total),) * 2, f32)],
    )
    far_parts = lax.ppermute(row_parts, Z0, [(0, 1), (1, 0)])
    row_parts = lax.all_gather(jnp.stack([row_parts, far_parts]), (XH, CORE), axis=0, tiled=False)
    col_parts = exchange(col_parts, COL_GROUP, col_groups())
    grads, totals, row_loss, base = call(
        own_kernel,
        (
            jax.ShapeDtypeStruct((rows_n, row_count, width), f32),
            jax.ShapeDtypeStruct((1, row_count), f32),
            jax.ShapeDtypeStruct((1, row_count), f32),
            jax.ShapeDtypeStruct((row_count, width), f32),
        ),
        rows, cols, row_parts, own, partner, positive,
        flops=4 * area * width, transcendentals=area,
        scratch=[pltpu.VMEM((rows_total // 128, 128), f32)],
    )
    halves = [
        call(
            functools.partial(side_kernel, flip),
            jax.ShapeDtypeStruct((rows_n // 2, row_count, width), f32),
            rows, cols, col_parts, grads,
            flops=2 * area * width, transcendentals=area // 2,
        )
        for flip in (1, 0)
    ]
    received = lax.ppermute(halves[0], CORE, [(0, 1), (1, 0)])
    grads = exchange(halves[1] + received, (XH, Z0))
    gradients = call(sum_kernel, jax.ShapeDtypeStruct((row_count, width), f32), grads, base)
    return (gradients[None], totals, row_loss)


def solution(mesh):
    view, batch = mesh.shape["view"], mesh.shape["batch"]
    inner = Mesh(
        mesh.devices.reshape(2, view // 2, 2, batch // 8, 2, 2), (PAIR, REST, XH, ZP, Z0, CORE)
    )
    v, b = (PAIR, REST), (XH, ZP, Z0, CORE)
    return jax.shard_map(
        step,
        mesh=inner,
        in_specs=(P(v, b, None), P(None, b)),
        out_specs=(P(v, b, None), P(v, b), P(v, b)),
        check_vma=False,
    )
```

```python
import jax
import jax.numpy as jnp
from jax import lax
from jax.experimental import pallas as pl
from jax.experimental.pallas import tpu as pltpu
from jax.sharding import Mesh, PartitionSpec as P


logit_scale = 10.0
log2_e = 1.4426950408889634
ln_2 = 0.6931471805599453

PAIR, REST = "pair", "rest"
XH, ZP, Z0, CORE = "xh", "zp", "z0", "core"
ROW_GROUP = (XH, Z0)
COL_GROUP = (ZP, CORE)
FLIP = [(0, 1), (1, 0)]
VMEM = pl.BlockSpec(memory_space=pltpu.VMEM)


def score_block(rows, cols):
    return lax.dot_general(
        rows, cols, (((1,), (1,)), ((), ())), preferred_element_type=jnp.float32
    ) * (logit_scale * log2_e)


def combine(parts):
    top = jnp.max(parts, axis=0)
    return top + jnp.log(jnp.sum(jnp.exp2(parts - top[None]), axis=0)) * log2_e


def column_group():
    return lax.rem(lax.axis_index(ZP) + lax.axis_index(CORE), lax.axis_size(CORE))


def to_tile(row):
    return jnp.concatenate([row[:, i : i + 128] for i in range(0, row.shape[1], 128)], axis=0)


def lse_over_left(left, right, score_ref):
    count, width = left.shape[0], right.shape[0]
    step = 512
    top = jnp.full((8, width), -1e30, jnp.float32)
    for start in range(0, count, step):
        block = score_block(left[start : start + step, :], right[...])
        score_ref[start : start + step, :width] = block
        top = jnp.maximum(top, jnp.max(block.reshape(step // 8, 8, width), axis=0))
    top = jnp.max(top, axis=0, keepdims=True)
    total = jnp.zeros((8, width), jnp.float32)
    for start in range(0, count, step):
        block = jnp.exp2(score_ref[start : start + step, :width] - top)
        total = total + jnp.sum(block.reshape(step // 8, 8, width), axis=0)
    return top + jnp.log(jnp.sum(total, axis=0, keepdims=True)) * log2_e


def near_lse_kernel(row_ref, col_ref, row_lse_ref, col_lse_ref, score_ref):
    col_lse_ref[...] = to_tile(lse_over_left(row_ref, col_ref, score_ref))
    row_lse_ref[...] = to_tile(lse_over_left(col_ref, row_ref, score_ref))


def far_lse_kernel(row_ref, col_ref, near_row_ref, near_col_ref, row_lse_ref, col_lse_ref, score_ref):
    far = to_tile(lse_over_left(row_ref, col_ref, score_ref))
    row_lse_ref[0] = near_row_ref[...]
    row_lse_ref[1] = to_tile(lse_over_left(col_ref, row_ref, score_ref))
    tile_rows = far.shape[0]
    group = column_group()
    near = near_col_ref[...]
    first = jnp.where(group == 0, near, far)
    second = jnp.where(group == 0, far, near)
    for peer in range(col_lse_ref.shape[0]):
        col_lse_ref[peer, :tile_rows, :] = first
        col_lse_ref[peer, tile_rows:, :] = second


def own_kernel(
    row_ref, near_ref, far_ref, parts_ref, own_ref, partner_ref, positive_ref,
    grad_ref, totals_ref, loss_ref, base_ref, totals_scratch,
):
    groups, halves, blocks, block_rows = parts_ref.shape
    totals = combine(parts_ref[...].reshape(groups * halves, blocks, block_rows))
    totals_scratch[:blocks, :] = totals
    shift = jnp.concatenate(
        [
            jnp.broadcast_to(totals[i : i + 1, :], (128, block_rows)).T for i in range(blocks)
        ],
        axis=0,
    )
    shift = jnp.concatenate([shift] * (near_ref.shape[0] // 128), axis=1)
    part = None
    for cols in (near_ref, far_ref):
        weights = jnp.exp2(score_block(row_ref[...], cols[...]) - shift)
        more = jnp.dot(
            weights.astype(jnp.bfloat16), cols[...], preferred_element_type=jnp.float32
        )
        part = more if part is None else part + more
    grad_ref[...] = part.reshape(grad_ref.shape)
    rest_count = lax.axis_size(REST)
    pair = lax.axis_index(PAIR)
    view = pair * rest_count + lax.axis_index(REST)
    far = (1 - pair) * rest_count + lax.axis_index(REST)
    own_match = positive_ref[pl.ds(view, 1), :]
    far_match = positive_ref[pl.ds(far, 1), :]
    row_ids = lax.broadcasted_iota(jnp.int32, (block_rows, block_rows), 0)
    own_hot = (row_ids == own_match).astype(jnp.float32).astype(jnp.bfloat16)
    far_hot = (row_ids == far_match).astype(jnp.float32).astype(jnp.bfloat16)
    partner = partner_ref[...]
    pos_rows = lax.dot_general(
        own_hot, partner, (((0,), (0,)), ((), ())), preferred_element_type=jnp.float32
    )
    matched = jnp.dot(far_hot, partner, preferred_element_type=jnp.float32)
    base_ref[...] = (pos_rows + matched) * -logit_scale
    product = own_ref[...].astype(jnp.float32) * pos_rows
    pos_score = jnp.sum(product.T, axis=0, keepdims=True) * logit_scale
    place = lax.axis_index(XH) * lax.axis_size(Z0) + lax.axis_index(Z0)
    own_totals = totals_scratch[pl.ds(place, 1), :] * ln_2
    totals_ref[...] = own_totals
    loss_ref[...] = own_totals - pos_score


def side_kernel(row_ref, near_ref, far_ref, parts_ref, own_grad_ref, grad_ref):
    totals = combine(parts_ref[...])
    half = totals.shape[0] // 2
    group = column_group()
    part = own_grad_ref[...].reshape(row_ref.shape[0], -1)
    for cols, flip in ((near_ref, 0), (far_ref, 1)):
        mine = jnp.where(jnp.bitwise_xor(group, flip) == 0, totals[:half, :], totals[half:, :])
        shift = jnp.concatenate([mine[i : i + 1, :] for i in range(half)], axis=1)
        weights = jnp.exp2(score_block(row_ref[...], cols[...]) - shift)
        part = part + jnp.dot(
            weights.astype(jnp.bfloat16), cols[...], preferred_element_type=jnp.float32
        )
    grad_ref[...] = part.reshape(grad_ref.shape)


def sum_kernel(parts_ref, base_ref, out_ref):
    total = parts_ref[0]
    for i in range(1, parts_ref.shape[0]):
        total = total + parts_ref[i]
    out_ref[...] = total * logit_scale + base_ref[...]


def call(kernel, outs, *args, flops=0, transcendentals=0, scratch=()):
    single = not isinstance(outs, tuple)
    out_list = (outs,) if single else outs
    moved = sum(a.size * a.dtype.itemsize for a in args)
    moved += sum(o.size * o.dtype.itemsize for o in out_list)
    return pl.pallas_call(
        kernel,
        out_shape=outs,
        in_specs=[VMEM] * len(args),
        out_specs=VMEM if single else tuple([VMEM] * len(out_list)),
        scratch_shapes=list(scratch),
        compiler_params=pltpu.CompilerParams(vmem_limit_bytes=16 << 20),
        cost_estimate=pl.CostEstimate(
            flops=flops, bytes_accessed=moved, transcendentals=transcendentals
        ),
    )(*args)


def col_groups():
    planes, cores = lax.axis_size(ZP), lax.axis_size(CORE)
    return [[p * cores + (p + g) % cores for p in range(planes)] for g in range(cores)]


def exchange(value, axes, groups=None):
    return lax.all_to_all(value, axes, 0, 0, tiled=True, axis_index_groups=groups)


def step(embeddings, positive):
    own = embeddings[0]
    row_count, width = own.shape
    rows_n = lax.axis_size(XH) * lax.axis_size(Z0)
    cols_n = lax.axis_size(ZP) * lax.axis_size(CORE)
    f32, shape = jnp.float32, jax.ShapeDtypeStruct
    partner = lax.ppermute(own, PAIR, FLIP)
    rows = exchange(jnp.broadcast_to(own[None], (rows_n, row_count, width)), ROW_GROUP)
    rows = rows.reshape(rows_n * row_count, width)
    near = lax.all_gather(partner, COL_GROUP, axis=0, tiled=True, axis_index_groups=col_groups())
    far = lax.ppermute(near, CORE, FLIP)
    row_tiles, col_tiles = rows.shape[0] // 128, near.shape[0] // 128
    area = rows.shape[0] * near.shape[0]
    scratch = [pltpu.VMEM((max(rows.shape[0], near.shape[0]),) * 2, f32)]
    near_row, near_col = call(
        near_lse_kernel,
        (shape((row_tiles, 128), f32), shape((col_tiles, 128), f32)),
        rows, near,
        flops=4 * area * width, transcendentals=2 * area, scratch=scratch,
    )
    row_parts, col_parts = call(
        far_lse_kernel,
        (shape((2, row_tiles, 128), f32), shape((cols_n, 2 * col_tiles, 128), f32)),
        rows, far, near_row, near_col,
        flops=4 * area * width, transcendentals=2 * area, scratch=scratch,
    )
    row_parts = lax.all_gather(row_parts, ROW_GROUP, axis=0, tiled=False)
    col_parts = exchange(col_parts, COL_GROUP)
    grads, totals, row_loss, base = call(
        own_kernel,
        (
            shape((rows_n, row_count, width), f32),
            shape((1, row_count), f32),
            shape((1, row_count), f32),
            shape((row_count, width), f32),
        ),
        rows, near, far, row_parts, own, partner, positive,
        flops=8 * area * width, transcendentals=2 * area,
        scratch=[pltpu.VMEM((8, 128), f32)],
    )
    grads = call(
        side_kernel,
        shape((rows_n, row_count, width), f32),
        rows, near, far, col_parts, grads,
        flops=8 * area * width, transcendentals=2 * area,
    )
    grads = exchange(grads, ROW_GROUP)
    gradients = call(sum_kernel, shape((row_count, width), f32), grads, base)
    return (gradients[None], totals, row_loss)


def solution(mesh):
    view, batch = mesh.shape["view"], mesh.shape["batch"]
    inner = Mesh(
        mesh.devices.reshape(2, view // 2, 2, batch // 8, 2, 2), (PAIR, REST, XH, ZP, Z0, CORE)
    )
    v, b = (PAIR, REST), (XH, ZP, Z0, CORE)
    return jax.shard_map(
        step,
        mesh=inner,
        in_specs=(P(v, b, None), P(None, b)),
        out_specs=(P(v, b, None), P(v, b), P(v, b)),
        check_vma=False,
    )
```

```python
import functools

import jax
import jax.numpy as jnp
from jax import lax
from jax.experimental import pallas as pl
from jax.experimental.pallas import tpu as pltpu
from jax.sharding import Mesh, PartitionSpec as P


logit_scale = 10.0
log2_e = 1.4426950408889634
ln_2 = 0.6931471805599453

PAIR, REST = "pair", "rest"
XH, ZP, Z0, CORE = "xh", "zp", "z0", "core"
ROW_GROUP = (XH, Z0)
COL_GROUP = (ZP, CORE)
FLIP = [(0, 1), (1, 0)]
VMEM = pl.BlockSpec(memory_space=pltpu.VMEM)


def score_block(rows, cols):
    return lax.dot_general(
        rows, cols, (((1,), (1,)), ((), ())), preferred_element_type=jnp.float32
    ) * (logit_scale * log2_e)


def combine(parts):
    top = jnp.max(parts, axis=0)
    return top + jnp.log(jnp.sum(jnp.exp2(parts - top[None]), axis=0)) * log2_e


def column_group():
    return lax.rem(lax.axis_index(ZP) + lax.axis_index(CORE), lax.axis_size(CORE))


def to_tile(row):
    return jnp.concatenate([row[:, i : i + 128] for i in range(0, row.shape[1], 128)], axis=0)


def lse_over_left(left, right, score_ref):
    count, width = left.shape[0], right.shape[0]
    step = 512
    top = jnp.full((8, width), -1e30, jnp.float32)
    for start in range(0, count, step):
        block = score_block(left[start : start + step, :], right[...])
        score_ref[start : start + step, :width] = block
        top = jnp.maximum(top, jnp.max(block.reshape(step // 8, 8, width), axis=0))
    top = jnp.max(top, axis=0, keepdims=True)
    total = jnp.zeros((8, width), jnp.float32)
    for start in range(0, count, step):
        block = jnp.exp2(score_ref[start : start + step, :width] - top)
        total = total + jnp.sum(block.reshape(step // 8, 8, width), axis=0)
    return top + jnp.log(jnp.sum(total, axis=0, keepdims=True)) * log2_e


def near_lse_kernel(row_ref, col_ref, row_lse_ref, col_lse_ref, score_ref):
    col_lse_ref[...] = to_tile(lse_over_left(row_ref, col_ref, score_ref))
    row_lse_ref[...] = to_tile(lse_over_left(col_ref, row_ref, score_ref))


def far_lse_kernel(row_ref, col_ref, near_row_ref, near_col_ref, row_lse_ref, col_lse_ref, score_ref):
    far = to_tile(lse_over_left(row_ref, col_ref, score_ref))
    row_lse_ref[0] = near_row_ref[...]
    row_lse_ref[1] = to_tile(lse_over_left(col_ref, row_ref, score_ref))
    tile_rows = far.shape[0]
    group = column_group()
    near = near_col_ref[...]
    first = jnp.where(group == 0, near, far)
    second = jnp.where(group == 0, far, near)
    for peer in range(col_lse_ref.shape[0]):
        col_lse_ref[peer, :tile_rows, :] = first
        col_lse_ref[peer, tile_rows:, :] = second


def own_kernel(
    row_ref, near_ref, far_ref, parts_ref, own_ref, partner_ref, positive_ref,
    grad_ref, totals_ref, loss_ref, base_ref, totals_scratch,
):
    groups, halves, blocks, block_rows = parts_ref.shape
    totals = combine(parts_ref[...].reshape(groups * halves, blocks, block_rows))
    totals_scratch[:blocks, :] = totals
    shift = jnp.concatenate(
        [
            jnp.broadcast_to(totals[i : i + 1, :], (128, block_rows)).T for i in range(blocks)
        ],
        axis=0,
    )
    shift = jnp.concatenate([shift] * (near_ref.shape[0] // 128), axis=1)
    part = None
    for cols in (near_ref, far_ref):
        weights = jnp.exp2(score_block(row_ref[...], cols[...]) - shift)
        more = jnp.dot(
            weights.astype(jnp.bfloat16), cols[...], preferred_element_type=jnp.float32
        )
        part = more if part is None else part + more
    grad_ref[...] = part.reshape(grad_ref.shape)
    rest_count = lax.axis_size(REST)
    pair = lax.axis_index(PAIR)
    view = pair * rest_count + lax.axis_index(REST)
    far = (1 - pair) * rest_count + lax.axis_index(REST)
    own_match = positive_ref[pl.ds(view, 1), :]
    far_match = positive_ref[pl.ds(far, 1), :]
    row_ids = lax.broadcasted_iota(jnp.int32, (block_rows, block_rows), 0)
    own_hot = (row_ids == own_match).astype(jnp.float32).astype(jnp.bfloat16)
    far_hot = (row_ids == far_match).astype(jnp.float32).astype(jnp.bfloat16)
    partner = partner_ref[...]
    pos_rows = lax.dot_general(
        own_hot, partner, (((0,), (0,)), ((), ())), preferred_element_type=jnp.float32
    )
    matched = jnp.dot(far_hot, partner, preferred_element_type=jnp.float32)
    base_ref[...] = (pos_rows + matched) * -logit_scale
    product = own_ref[...].astype(jnp.float32) * pos_rows
    pos_score = jnp.sum(product.T, axis=0, keepdims=True) * logit_scale
    place = lax.axis_index(XH) * lax.axis_size(Z0) + lax.axis_index(Z0)
    own_totals = totals_scratch[pl.ds(place, 1), :] * ln_2
    totals_ref[...] = own_totals
    loss_ref[...] = own_totals - pos_score


def side_kernel(picks, row_ref, near_ref, far_ref, parts_ref, own_grad_ref, *grad_refs):
    totals = combine(parts_ref[...])
    half = totals.shape[0] // 2
    group = column_group()
    block_rows = own_grad_ref.shape[1]
    here = lax.axis_index(XH) * lax.axis_size(Z0) + lax.axis_index(Z0)
    blocks = [jnp.bitwise_xor(here, i) for i in picks]
    rows = jnp.concatenate(
        [row_ref[pl.ds(pl.multiple_of(k * block_rows, block_rows), block_rows), :] for k in blocks],
        axis=0,
    )
    part = jnp.concatenate([own_grad_ref[k] for k in blocks], axis=0)
    for cols, flip in ((near_ref, 0), (far_ref, 1)):
        mine = jnp.where(jnp.bitwise_xor(group, flip) == 0, totals[:half, :], totals[half:, :])
        shift = jnp.concatenate([mine[i : i + 1, :] for i in range(half)], axis=1)
        weights = jnp.exp2(score_block(rows, cols[...]) - shift)
        part = part + jnp.dot(
            weights.astype(jnp.bfloat16), cols[...], preferred_element_type=jnp.float32
        )
    for i, out in enumerate(grad_refs):
        out[...] = part[i * block_rows : (i + 1) * block_rows, :]


def sum_kernel(own_ref, z0_ref, xh_ref, both_ref, base_ref, out_ref):
    total = (own_ref[...] + z0_ref[...]) + (xh_ref[...] + both_ref[...])
    out_ref[...] = total * logit_scale + base_ref[...]


def call(kernel, outs, *args, flops=0, transcendentals=0, scratch=()):
    single = not isinstance(outs, tuple)
    out_list = (outs,) if single else outs
    moved = sum(a.size * a.dtype.itemsize for a in args)
    moved += sum(o.size * o.dtype.itemsize for o in out_list)
    return pl.pallas_call(
        kernel,
        out_shape=outs,
        in_specs=[VMEM] * len(args),
        out_specs=VMEM if single else tuple([VMEM] * len(out_list)),
        scratch_shapes=list(scratch),
        compiler_params=pltpu.CompilerParams(vmem_limit_bytes=16 << 20),
        cost_estimate=pl.CostEstimate(
            flops=flops, bytes_accessed=moved, transcendentals=transcendentals
        ),
    )(*args)


def col_groups():
    planes, cores = lax.axis_size(ZP), lax.axis_size(CORE)
    return [[p * cores + (p + g) % cores for p in range(planes)] for g in range(cores)]


def exchange(value, axes, groups=None):
    return lax.all_to_all(value, axes, 0, 0, tiled=True, axis_index_groups=groups)


def step(embeddings, positive):
    own = embeddings[0]
    row_count, width = own.shape
    rows_n = lax.axis_size(XH) * lax.axis_size(Z0)
    cols_n = lax.axis_size(ZP) * lax.axis_size(CORE)
    f32, shape = jnp.float32, jax.ShapeDtypeStruct
    partner = lax.ppermute(own, PAIR, FLIP)
    rows = exchange(jnp.broadcast_to(own[None], (rows_n, row_count, width)), ROW_GROUP)
    rows = rows.reshape(rows_n * row_count, width)
    near = lax.all_gather(partner, COL_GROUP, axis=0, tiled=True, axis_index_groups=col_groups())
    far = lax.ppermute(near, CORE, FLIP)
    row_tiles, col_tiles = rows.shape[0] // 128, near.shape[0] // 128
    area = rows.shape[0] * near.shape[0]
    scratch = [pltpu.VMEM((max(rows.shape[0], near.shape[0]),) * 2, f32)]
    near_row, near_col = call(
        near_lse_kernel,
        (shape((row_tiles, 128), f32), shape((col_tiles, 128), f32)),
        rows, near,
        flops=4 * area * width, transcendentals=2 * area, scratch=scratch,
    )
    row_parts, col_parts = call(
        far_lse_kernel,
        (shape((2, row_tiles, 128), f32), shape((cols_n, 2 * col_tiles, 128), f32)),
        rows, far, near_row, near_col,
        flops=4 * area * width, transcendentals=2 * area, scratch=scratch,
    )
    row_parts = lax.all_gather(row_parts, ROW_GROUP, axis=0, tiled=False)
    col_parts = exchange(col_parts, COL_GROUP)
    grads, totals, row_loss, base = call(
        own_kernel,
        (
            shape((rows_n, row_count, width), f32),
            shape((1, row_count), f32),
            shape((1, row_count), f32),
            shape((row_count, width), f32),
        ),
        rows, near, far, row_parts, own, partner, positive,
        flops=8 * area * width, transcendentals=2 * area,
        scratch=[pltpu.VMEM((8, 128), f32)],
    )

    def side(picks):
        return call(
            functools.partial(side_kernel, picks),
            (shape((row_count, width), f32), shape((row_count, width), f32)),
            rows, near, far, col_parts, grads,
            flops=4 * area * width, transcendentals=area,
        )

    both, across = side((3, 2))
    both = lax.ppermute(both, (XH, Z0), [(0, 3), (1, 2), (2, 1), (3, 0)])
    across = lax.ppermute(across, XH, FLIP)
    beside, kept = side((1, 0))
    beside = lax.ppermute(beside, Z0, FLIP)
    gradients = call(
        sum_kernel, shape((row_count, width), f32), kept, beside, across, both, base
    )
    return (gradients[None], totals, row_loss)


def solution(mesh):
    view, batch = mesh.shape["view"], mesh.shape["batch"]
    inner = Mesh(
        mesh.devices.reshape(2, view // 2, 2, batch // 8, 2, 2), (PAIR, REST, XH, ZP, Z0, CORE)
    )
    v, b = (PAIR, REST), (XH, ZP, Z0, CORE)
    return jax.shard_map(
        step,
        mesh=inner,
        in_specs=(P(v, b, None), P(None, b)),
        out_specs=(P(v, b, None), P(v, b), P(v, b)),
        check_vma=False,
    )
```
